32 devices in a mesh: pair: 4 (over y, x), virt: 8 (over z, core).
Axes of the slice: x: 2, y: 2, z: 4, core: 2. Of those that a mesh axis runs over, the one named last changes fastest.
Arguments:
- amplitudes: float32 [480, 12288], P('pair', 'virt'), may hold values from -6 to 6
- integrals: float32 [8192, 12288], P('pair', 'virt'), may hold values from -0.0546875 to 0.0546875
- eps_occ: float32 [120], replicated, may hold values from -2.5 to -0.3
- eps_vir: float32 [128], replicated, may hold values from 0.3 to 3
- pair_list: int32 [480, 2], P('pair'), may hold values from 0 to 119, as said below
Outputs:
- ladder: float32 [480, 8192], P('pair', 'virt')
- update: float32 [480, 8192], P('pair', 'virt')
The draws below stay inside these ranges and needn't reach their ends.
Inputs may be any that keep to these rules, and one draw needn't show every extreme that they name: `pair_list`: each row (i, j) has i < j; pairs may repeat.
All inputs are finite; a program needn't handle non-finite values.
Results may differ from the reference program's by a relative error of at most 0.000071.
Values sent between devices are 32-bit elements; how exact they have to be, the bound alone decides.
A program may use at most 64 MiB of HBM per device.

```python
import jax
import jax.numpy as jnp
from jax import lax

TILE = 64
NOCC = 120
PAIRS = 480
NVT = 128
AB = 8192
CD = 12288


def draw_pair_list(key, part):
    first_key, second_key, place_key = jax.random.split(jax.random.fold_in(key, 17), 3)
    smaller = jax.random.randint(first_key, (PAIRS,), 0, NOCC - 1)
    offsets = jax.random.randint(second_key, (PAIRS,), 0, 1 << 20)
    larger = smaller + 1 + offsets % (NOCC - 1 - smaller)
    where_full = jax.random.randint(place_key, (), 0, PAIRS)
    row_ids = jnp.arange(PAIRS)
    smaller = jnp.where(row_ids == where_full, 0, smaller)
    larger = jnp.where(row_ids == where_full, NOCC - 1, larger)
    return jnp.stack([smaller, larger], axis=1).astype(jnp.int32)


def level_of(stream_key, extent, cuts, least, high):
    def one(axis_at, shards_of):
        heights = jax.random.uniform(jax.random.fold_in(jax.random.fold_in(stream_key, 6), axis_at), (shards_of,), jnp.float32, least / len(cuts), high / len(cuts))
        return jnp.repeat(jnp.exp(heights), extent[axis_at] // shards_of).reshape((-1,) + (1,) * (len(extent) - axis_at - 1))

    gain = one(*cuts[0])
    for cut in cuts[1:]:
        gain = gain * one(*cut)
    return gain


def bell_draw(stream_key, extent, spread, most, pieces=(), dtype=jnp.bfloat16):
    array = jax.random.normal(stream_key, extent, jnp.float32) * spread
    if len(pieces) > 0:
        array = level_of(stream_key, extent, pieces, -0.22, 0.18) * array
    return jnp.clip(array, min=-most, max=most).astype(dtype)


def setup_inputs(seed: int = 0) -> dict:
    key_of = jax.random.split(jax.random.key(seed), 6)
    amplitudes = bell_draw(key_of[0], (PAIRS, CD), 1.0, 6.0, ((0, 4), (1, 8)), jnp.float32)
    integrals = bell_draw(key_of[1], (AB, CD), CD ** -0.5, 0.0546875, ((0, 4), (1, 8)), jnp.float32)
    eps_occ = jnp.clip(jax.random.uniform(key_of[2], (NOCC,), jnp.float32, -2.5, -0.3), -2.5, -0.3)
    eps_vir = jnp.clip(jax.random.uniform(key_of[3], (NVT,), jnp.float32, 0.3, 3.0), 0.3, 3.0)
    pair_list = draw_pair_list(jax.random.fold_in(key_of[5], 71), 0)
    return dict(amplitudes=amplitudes, integrals=integrals, eps_occ=eps_occ, eps_vir=eps_vir, pair_list=pair_list)


def reference(amplitudes, integrals, eps_occ, eps_vir, pair_list):
    ladder_raw = lax.dot_general(amplitudes, integrals, (((1,), (1,)), ((), ())), precision=lax.Precision.HIGHEST, preferred_element_type=jnp.float32)
    blocks = ladder_raw.reshape(PAIRS, 2, TILE, TILE)
    mirrored = jnp.swapaxes(blocks[:, ::-1], 2, 3)
    ladder = (blocks - mirrored).reshape(PAIRS, AB)
    pair_energy = eps_occ[pair_list[:, 0]] + eps_occ[pair_list[:, 1]]
    energy_tiles = eps_vir.reshape(2, TILE)
    virt_energy = (energy_tiles[:, :, None] + energy_tiles[::-1][:, None, :]).reshape(AB)
    update = ladder / (pair_energy[:, None] - virt_energy[None, :])
    return ladder, update
```

```python
import functools

import jax
import jax.numpy as jnp
from jax import lax
from jax.experimental import pallas as pl
from jax.experimental.pallas import tpu as pltpu
from jax.sharding import PartitionSpec as P

MESH = pl.DeviceIdType.MESH
LANES = 128


def antisymmetrize(partial_value, tile_width):
    blocks = partial_value.reshape(partial_value.shape[0], 2, tile_width, tile_width)
    mirrored = jnp.swapaxes(blocks[:, ::-1], 2, 3)
    return (blocks - mirrored).reshape(partial_value.shape)


def pair_energies(eps_occ, pair_list):
    occ_ids = lax.broadcasted_iota(jnp.int32, (1, 1, eps_occ.shape[0]), 2)
    one_hot = pair_list[:, :, None] == occ_ids
    return jnp.sum(jnp.where(one_hot, eps_occ[None, None, :], jnp.float32(0.0)), axis=(1, 2))


def sum_to_owners(antisym):
    return lax.psum_scatter(antisym, "virt", scatter_dimension=1, tiled=True)


def updated(ladder, eps_occ, eps_vir, pair_list):
    tile_width = eps_vir.shape[0] // 2
    column_count = ladder.shape[1]
    energy_tiles = eps_vir.reshape(2, tile_width)
    virt_energy = (energy_tiles[:, :, None] + energy_tiles[::-1][:, None, :]).reshape(
        2 * tile_width * tile_width
    )
    local_energy = lax.dynamic_slice_in_dim(
        virt_energy, lax.axis_index("virt") * column_count, column_count
    )
    pair_energy = pair_energies(eps_occ, pair_list)
    return ladder / (pair_energy[:, None] - local_energy[None, :])


def any_mesh_body(amplitudes, integrals, eps_occ, eps_vir, pair_list):
    tile_width = eps_vir.shape[0] // 2
    by_pairs = lax.dot_general(
        lax.all_gather(amplitudes, "pair", axis=0, tiled=True),
        integrals,
        (((1,), (1,)), ((), ())),
        precision=lax.Precision.HIGHEST,
        preferred_element_type=jnp.float32,
    )
    partial_value = lax.all_to_all(by_pairs, "pair", split_axis=0, concat_axis=1, tiled=True)
    ladder = sum_to_owners(antisymmetrize(partial_value, tile_width))
    return (ladder, updated(ladder, eps_occ, eps_vir, pair_list))


def reduce_kernel(
    h, ct_ref, out_ref, got, summed, rows, diff, below, above, upward, downward, kept, other,
    core_send, core_recv, pair_send, pair_recv, up_send, up_recv, down_send, down_recv,
    last_send, last_recv,
):
    r = lax.axis_index("pair")
    v = lax.axis_index("virt")
    z = v // 2
    c = v % 2
    mate = v + 1 - 2 * c
    x = r % 2
    y = r // 2
    peers = (y * 2 + (1 - x), (1 - y) * 2 + x, (1 - y) * 2 + (1 - x))
    quad = 2 * h * h

    barrier = pltpu.get_barrier_semaphore()
    pl.semaphore_signal(barrier, inc=1, device_id={"virt": mate}, device_id_type=MESH)
    for peer in peers:
        pl.semaphore_signal(barrier, inc=1, device_id={"pair": peer}, device_id_type=MESH)

    @pl.when(z < 3)
    def _():
        pl.semaphore_signal(barrier, inc=1, device_id={"virt": v + 2}, device_id_type=MESH)

    @pl.when(z > 0)
    def _():
        pl.semaphore_signal(barrier, inc=1, device_id={"virt": v - 2}, device_id_type=MESH)

    inner = jnp.logical_and(z > 0, z < 3)

    @pl.when(inner)
    def _():
        pl.semaphore_wait(barrier, 6)

    @pl.when(jnp.logical_not(inner))
    def _():
        pl.semaphore_wait(barrier, 5)

    order = (peers[2], peers[0], peers[1], r)

    def core_copy(n, i):
        lanes = pl.ds(pl.multiple_of(order[n] * LANES, LANES), LANES)
        return pltpu.make_async_remote_copy(
            src_ref=ct_ref.at[i, :, :, (1 - c + i) % 2, :, lanes],
            dst_ref=got.at[n, i],
            send_sem=core_send.at[n, i],
            recv_sem=core_recv.at[n, i],
            device_id={"virt": mate},
            device_id_type=MESH,
        )

    def pair_copy(n):
        return pltpu.make_async_remote_copy(
            src_ref=summed.at[n],
            dst_ref=rows.at[pl.ds(pl.multiple_of(r * 2 * quad, 8), 2 * quad)],
            send_sem=pair_send.at[n],
            recv_sem=pair_recv.at[n],
            device_id={"pair": order[n]},
            device_id_type=MESH,
        )

    for n in range(4):
        for i in range(2):
            core_copy(n, i).start()
    for n in range(4):
        lanes = pl.ds(pl.multiple_of(order[n] * LANES, LANES), LANES)
        for i in range(2):
            core_copy(n, i).wait_recv()

            @pl.loop(0, h)
            def _(a):
                for bh in range(2):
                    total = ct_ref[i, a, bh, (c + i) % 2, :, lanes] + got[n, i, a, bh]
                    start = ((i * h + a) * 2 + bh) * h
                    if n < 3:
                        summed[n, pl.ds(pl.multiple_of(start, 8), h), :] = total
                    else:
                        at = pl.multiple_of(r * 2 * quad + start, 8)
                        rows[pl.ds(at, h), :] = total

        if n < 3:
            pair_copy(n).start()

    for n in range(3):
        pair_copy(n).wait_recv()

    for ah in range(2):
        for bh in range(2):
            for i in range(2):

                @pl.loop(0, h)
                def _(a):
                    mirror = (c + i) % 2
                    direct = (((ah * 2 + i) * h + a) * 2 + bh) * h
                    swapped = ((((2 + bh) * 2 + mirror) * h) * 2 + ah) * h + a
                    plain = rows[pl.ds(pl.multiple_of(direct, 8), h), :]
                    turned = rows[pl.ds(swapped, h, stride=2 * h), :]
                    at = pl.multiple_of((i * h + a) * h, 8)
                    diff[ah * 2 + bh, pl.ds(at, h), :] = plain - turned

    def up_copy(q):
        return pltpu.make_async_remote_copy(
            src_ref=upward.at[q], dst_ref=below.at[q],
            send_sem=up_send.at[q], recv_sem=up_recv.at[q],
            device_id={"virt": v + 2}, device_id_type=MESH,
        )

    def down_copy(q):
        return pltpu.make_async_remote_copy(
            src_ref=downward.at[q], dst_ref=above.at[q],
            send_sem=down_send.at[q], recv_sem=down_recv.at[q],
            device_id={"virt": v - 2}, device_id_type=MESH,
        )

    def sends_up(q):
        return (z < 2) if q % 2 == 0 else (z < 3)

    def sends_down(q):
        return (z > 1) if q // 2 == 1 else (z > 0)

    def hears_below(q):
        return jnp.logical_and(z > 0, z < 3) if q % 2 == 0 else (z > 0)

    def hears_above(q):
        return jnp.logical_and(z > 0, z < 3) if q // 2 == 1 else (z < 3)

    def pass_up(q):
        @pl.when(z == 0)
        def _():
            upward[q] = diff[q]

        @pl.when(hears_below(q))
        def _():
            up_copy(q).wait_recv()

            @pl.when(sends_up(q))
            def _():
                upward[q] = diff[q] + below[q]

        @pl.when(sends_up(q))
        def _():
            up_copy(q).start()

    def pass_down(q):
        @pl.when(z == 3)
        def _():
            downward[q] = diff[q]

        @pl.when(hears_above(q))
        def _():
            down_copy(q).wait_recv()

            @pl.when(sends_down(q))
            def _():
                downward[q] = diff[q] + above[q]

        @pl.when(sends_down(q))
        def _():
            down_copy(q).start()

    quads = (1, 0, 3, 2)

    @pl.when(z < 2)
    def _():
        for s in range(5):
            if s < 4:
                pass_up(quads[s])
            if s > 0:
                pass_down(quads[s - 1])

    @pl.when(z >= 2)
    def _():
        for s in range(5):
            if s < 4:
                pass_down(quads[s])
            if s > 0:
                pass_up(quads[s - 1])

    def total_of(t, i):
        q = jnp.where(z < 2, z * 2 + t, t * 2 + z - 2)
        at = pl.ds(pl.multiple_of(i * h * h, 8), h * h)
        low = jnp.where(z > 0, below[q, at, :], jnp.float32(0.0))
        high = jnp.where(z < 3, above[q, at, :], jnp.float32(0.0))
        return diff[q, at, :] + low + high

    mine = jnp.where(z < 2, c, 0)
    for t in range(2):
        other[t] = total_of(t, jnp.where(z < 2, 1 - c, 1))
    last = pltpu.make_async_remote_copy(
        src_ref=other, dst_ref=kept.at[1], send_sem=last_send, recv_sem=last_recv,
        device_id={"virt": mate}, device_id_type=MESH,
    )
    last.start()
    for t in range(2):
        kept[0, t] = total_of(t, mine)

    def put(s):
        for t in range(2):

            @pl.loop(0, h)
            def _(a):
                at = pl.multiple_of((a * 4 + 2 * t + s) * h, 8)
                plain = kept[s, t, pl.ds(pl.multiple_of(a * h, 8), h), :]
                turned = kept[s, t, pl.ds(a, h, stride=h), :]
                out_ref[pl.ds(at, h), :] = jnp.where(z < 2, plain, -turned)

    put(0)
    last.wait_recv()
    put(1)

    last.wait_send()
    for n in range(4):
        for i in range(2):
            core_copy(n, i).wait_send()
    for n in range(3):
        pair_copy(n).wait_send()
    for q in range(4):

        @pl.when(sends_up(q))
        def _():
            up_copy(q).wait_send()

        @pl.when(sends_down(q))
        def _():
            down_copy(q).wait_send()


def reduced(ct, tile_width):
    h = tile_width // 4
    quad = 2 * h * h
    ct = ct.reshape(2, h, 2, 2, h, ct.shape[1])
    f32 = jnp.float32
    dma = pltpu.SemaphoreType.DMA
    return pl.pallas_call(
        functools.partial(reduce_kernel, h),
        out_shape=jax.ShapeDtypeStruct((tile_width * h, LANES), f32),
        in_specs=[pl.BlockSpec(memory_space=pltpu.VMEM)],
        out_specs=pl.BlockSpec(memory_space=pltpu.VMEM),
        scratch_shapes=[
            pltpu.VMEM((4, 2, h, 2, h, LANES), f32),
            pltpu.VMEM((3, 2 * quad, LANES), f32),
            pltpu.VMEM((8 * quad, LANES), f32),
            pltpu.VMEM((4, quad, LANES), f32),
            pltpu.VMEM((4, quad, LANES), f32),
            pltpu.VMEM((4, quad, LANES), f32),
            pltpu.VMEM((4, quad, LANES), f32),
            pltpu.VMEM((4, quad, LANES), f32),
            pltpu.VMEM((2, 2, h * h, LANES), f32),
            pltpu.VMEM((2, h * h, LANES), f32),
            dma((4, 2)), dma((4, 2)), dma((3,)), dma((3,)),
            dma((4,)), dma((4,)), dma((4,)), dma((4,)), dma, dma,
        ],
        compiler_params=pltpu.CompilerParams(
            collective_id=0, has_side_effects=True, vmem_limit_bytes=48 * 1024 * 1024
        ),
        name="reduce_antisymmetrized",
    )(ct)


def block_body(amplitudes, integrals, eps_occ, eps_vir, pair_list):
    tile_width = eps_vir.shape[0] // 2
    count = amplitudes.shape[0]
    gathered = lax.all_gather(amplitudes, "pair", axis=0, tiled=False)
    gathered = jnp.pad(gathered, ((0, 0), (0, LANES - count), (0, 0)))
    ct = lax.dot_general(
        integrals,
        gathered.reshape(-1, gathered.shape[2]),
        (((1,), (1,)), ((), ())),
        precision=lax.Precision.HIGH,
        preferred_element_type=jnp.float32,
    )
    ladder = reduced(ct, tile_width).T[:count]
    return (ladder, updated(ladder, eps_occ, eps_vir, pair_list))


def solution(mesh):
    in_specs = (P("pair", "virt"), P("pair", "virt"), P(), P(), P("pair", None))
    out_specs = (P("pair", "virt"), P("pair", "virt"))
    fits = mesh.shape["pair"] == 4 and mesh.shape["virt"] == 8

    def body(amplitudes, integrals, eps_occ, eps_vir, pair_list):
        tiled = eps_vir.shape[0] % 64 == 0 and amplitudes.shape[0] <= LANES
        chosen = block_body if fits and tiled else any_mesh_body
        return chosen(amplitudes, integrals, eps_occ, eps_vir, pair_list)

    return jax.shard_map(body, mesh=mesh, in_specs=in_specs, out_specs=out_specs, check_vma=False)
```

```python
import functools

import jax
import jax.numpy as jnp
from jax import lax
from jax.experimental import pallas as pl
from jax.experimental.pallas import tpu as pltpu
from jax.sharding import PartitionSpec as P

MESH = pl.DeviceIdType.MESH
LANES = 128


def antisymmetrize(partial_value, tile_width):
    blocks = partial_value.reshape(partial_value.shape[0], 2, tile_width, tile_width)
    mirrored = jnp.swapaxes(blocks[:, ::-1], 2, 3)
    return (blocks - mirrored).reshape(partial_value.shape)


def pair_energies(eps_occ, pair_list):
    occ_ids = lax.broadcasted_iota(jnp.int32, (1, 1, eps_occ.shape[0]), 2)
    one_hot = pair_list[:, :, None] == occ_ids
    return jnp.sum(jnp.where(one_hot, eps_occ[None, None, :], jnp.float32(0.0)), axis=(1, 2))


def sum_to_owners(antisym):
    return lax.psum_scatter(antisym, "virt", scatter_dimension=1, tiled=True)


def updated(ladder, eps_occ, eps_vir, pair_list):
    tile_width = eps_vir.shape[0] // 2
    column_count = ladder.shape[1]
    energy_tiles = eps_vir.reshape(2, tile_width)
    virt_energy = (energy_tiles[:, :, None] + energy_tiles[::-1][:, None, :]).reshape(
        2 * tile_width * tile_width
    )
    local_energy = lax.dynamic_slice_in_dim(
        virt_energy, lax.axis_index("virt") * column_count, column_count
    )
    pair_energy = pair_energies(eps_occ, pair_list)
    return ladder / (pair_energy[:, None] - local_energy[None, :])


def any_mesh_body(amplitudes, integrals, eps_occ, eps_vir, pair_list):
    tile_width = eps_vir.shape[0] // 2
    by_pairs = lax.dot_general(
        lax.all_gather(amplitudes, "pair", axis=0, tiled=True),
        integrals,
        (((1,), (1,)), ((), ())),
        precision=lax.Precision.HIGHEST,
        preferred_element_type=jnp.float32,
    )
    partial_value = lax.all_to_all(by_pairs, "pair", split_axis=0, concat_axis=1, tiled=True)
    ladder = sum_to_owners(antisymmetrize(partial_value, tile_width))
    return (ladder, updated(ladder, eps_occ, eps_vir, pair_list))


def split(value):
    high = value.astype(jnp.bfloat16)
    return high, (value - high.astype(jnp.float32)).astype(jnp.bfloat16)


def times(left, right):
    return lax.dot_general(
        left, right, (((1,), (1,)), ((), ())), preferred_element_type=jnp.float32
    )


def ladder_kernel(
    h, amp_ref, int_ref, out_ref, stage, int_high, int_low, blocks, weights, ct_ref,
    got, summed, rows, diff, below, above, upward, downward, kept, other,
    stage_sem, amp_send, amp_recv,
    core_send, core_recv, pair_send, pair_recv, up_send, up_recv, down_send, down_recv,
    last_send, last_recv,
):
    r = lax.axis_index("pair")
    v = lax.axis_index("virt")
    z = v // 2
    c = v % 2
    mate = v + 1 - 2 * c
    x = r % 2
    y = r // 2
    peers = (y * 2 + (1 - x), (1 - y) * 2 + x, (1 - y) * 2 + (1 - x))
    quad = 2 * h * h
    count, depth = amp_ref.shape
    cut = count // 16 * 8
    parts = (pl.ds(0, cut), pl.ds(cut, count - cut))
    step = stage.shape[1]
    steps = int_ref.shape[0] // step

    def stage_copy(t):
        return pltpu.make_async_copy(
            int_ref.at[pl.ds(pl.multiple_of(t * step, 8), step)],
            stage.at[t % 2],
            stage_sem.at[t % 2],
        )

    stage_copy(0).start()
    stage_copy(1).start()

    barrier = pltpu.get_barrier_semaphore()
    pl.semaphore_signal(barrier, inc=1, device_id={"virt": mate}, device_id_type=MESH)
    for peer in peers:
        pl.semaphore_signal(barrier, inc=1, device_id={"pair": peer}, device_id_type=MESH)

    @pl.when(z < 3)
    def _():
        pl.semaphore_signal(barrier, inc=1, device_id={"virt": v + 2}, device_id_type=MESH)

    @pl.when(z > 0)
    def _():
        pl.semaphore_signal(barrier, inc=1, device_id={"virt": v - 2}, device_id_type=MESH)

    inner = jnp.logical_and(z > 0, z < 3)

    @pl.when(inner)
    def _():
        pl.semaphore_wait(barrier, 6)

    @pl.when(jnp.logical_not(inner))
    def _():
        pl.semaphore_wait(barrier, 5)

    def amp_copy(d, part):
        return pltpu.make_async_remote_copy(
            src_ref=amp_ref.at[parts[part]],
            dst_ref=blocks.at[d, parts[part]],
            send_sem=amp_send.at[d, part],
            recv_sem=amp_recv.at[d, part],
            device_id={"pair": peers[d]},
            device_id_type=MESH,
        )

    def pass_on(d):
        return pltpu.make_async_remote_copy(
            src_ref=blocks.at[d, parts[d]],
            dst_ref=blocks.at[2, parts[d]],
            send_sem=amp_send.at[2, d],
            recv_sem=amp_recv.at[2, d],
            device_id={"pair": peers[1 - d]},
            device_id_type=MESH,
        )

    for late in range(2):
        for d in range(2):
            amp_copy(d, d if late == 0 else 1 - d).start()

    def weigh(source, high_at, low_at):
        wide = 2 * LANES

        @pl.loop(0, depth // wide)
        def _(k):
            columns = pl.ds(pl.multiple_of(k * wide, wide), wide)
            value = source[:, columns]
            if count < LANES:
                value = jnp.concatenate(
                    [value, jnp.zeros((LANES - count, wide), jnp.float32)], axis=0
                )
            high, low = split(value)
            weights[pl.ds(high_at * LANES, LANES), columns] = high
            weights[pl.ds(low_at * LANES, LANES), columns] = low

    def keep(t, size, lanes, value):
        per = size // (4 * h)
        i = t // (h // per)
        at = pl.multiple_of(t % (h // per) * per, per)
        ct_ref[i, pl.ds(at, per), :, :, :, lanes] = value.reshape(per, 2, 2, h, value.shape[1])

    def one_block(high, low, at):
        both = times(high, weights[pl.ds(at * LANES, 2 * LANES), :])
        rest = times(low, weights[pl.ds(at * LANES, LANES), :])
        return both[:, :LANES] + both[:, LANES:] + rest

    weigh(amp_ref, 0, 1)

    @pl.loop(0, steps)
    def _(t):
        stage_copy(t).wait()
        high, low = split(stage[t % 2])
        at = pl.ds(pl.multiple_of(t * step, 16), step)
        int_high[at, :] = high
        int_low[at, :] = low

        @pl.when(t + 2 < steps)
        def _():
            stage_copy(t + 2).start()

        keep(t, step, pl.ds(3 * LANES, LANES), one_block(int_high[at, :], int_low[at, :], 0))

    for d in range(2):
        amp_copy(d, d).wait_recv()
        pass_on(d).start()

    order = (peers[2], peers[0], peers[1], r)

    def core_copy(n, i):
        return pltpu.make_async_remote_copy(
            src_ref=ct_ref.at[i, :, :, (1 - c + i) % 2, :, pl.ds(n * LANES, LANES)],
            dst_ref=got.at[n, i],
            send_sem=core_send.at[n, i],
            recv_sem=core_recv.at[n, i],
            device_id={"virt": mate},
            device_id_type=MESH,
        )

    def pair_copy(n):
        return pltpu.make_async_remote_copy(
            src_ref=summed.at[n],
            dst_ref=rows.at[pl.ds(pl.multiple_of(r * 2 * quad, 8), 2 * quad)],
            send_sem=pair_send.at[n],
            recv_sem=pair_recv.at[n],
            device_id={"pair": order[n]},
            device_id_type=MESH,
        )

    def core_start(n):
        for i in range(2):
            core_copy(n, i).start()

    def core_add(n):
        lanes = pl.ds(n * LANES, LANES)
        for i in range(2):
            core_copy(n, i).wait_recv()

            @pl.loop(0, h)
            def _(a):
                for bh in range(2):
                    total = ct_ref[i, a, bh, (c + i) % 2, :, lanes] + got[n, i, a, bh]
                    start = ((i * h + a) * 2 + bh) * h
                    if n < 3:
                        summed[n, pl.ds(pl.multiple_of(start, 8), h), :] = total
                    else:
                        at = pl.multiple_of(r * 2 * quad + start, 8)
                        rows[pl.ds(at, h), :] = total

    core_start(3)
    for d in range(2):
        amp_copy(d, 1 - d).wait_recv()
        weigh(blocks.at[d], 4 + d, 6 + d)
    big = 2 * step

    @pl.loop(0, steps // 2)
    def _(t):
        at = pl.ds(pl.multiple_of(t * big, 16), big)
        near_high = weights[pl.ds(4 * LANES, 2 * LANES), :]
        near_low = weights[pl.ds(6 * LANES, 2 * LANES), :]
        value = times(int_high[at, :], near_high) + times(int_high[at, :], near_low)
        value = value + times(int_low[at, :], near_high)
        keep(t, big, pl.ds(LANES, 2 * LANES), value)

    core_start(1)
    core_start(2)
    core_add(3)
    for n in (1, 2):
        core_add(n)
        pair_copy(n).start()
    for d in range(2):
        pass_on(d).wait_recv()
    weigh(blocks.at[2], 2, 3)

    @pl.loop(0, steps // 2)
    def _(t):
        at = pl.ds(pl.multiple_of(t * big, 16), big)
        keep(t, big, pl.ds(0, LANES), one_block(int_high[at, :], int_low[at, :], 2))

    core_start(0)
    core_add(0)
    pair_copy(0).start()

    def antisym(q):
        ah = q // 2
        bh = q % 2
        for i in range(2):
            mirror = (c + i) % 2

            @pl.loop(0, h)
            def _(a):
                direct = (((ah * 2 + i) * h + a) * 2 + bh) * h
                swapped = ((((2 + bh) * 2 + mirror) * h) * 2 + ah) * h + a
                plain = rows[pl.ds(pl.multiple_of(direct, 8), h), :]
                turned = rows[pl.ds(swapped, h, stride=2 * h), :]
                at = pl.multiple_of((i * h + a) * h, 8)
                diff[q, pl.ds(at, h), :] = plain - turned

    def up_copy(q):
        return pltpu.make_async_remote_copy(
            src_ref=upward.at[q], dst_ref=below.at[q],
            send_sem=up_send.at[q], recv_sem=up_recv.at[q],
            device_id={"virt": v + 2}, device_id_type=MESH,
        )

    def down_copy(q):
        return pltpu.make_async_remote_copy(
            src_ref=downward.at[q], dst_ref=above.at[q],
            send_sem=down_send.at[q], recv_sem=down_recv.at[q],
            device_id={"virt": v - 2}, device_id_type=MESH,
        )

    def sends_up(q):
        return jnp.logical_or(z < 2, jnp.logical_and(z == 2, q % 2 == 1))

    def sends_down(q):
        return jnp.logical_or(z > 1, jnp.logical_and(z == 1, q // 2 == 0))

    def hears_below(q):
        return jnp.logical_or(inner, jnp.logical_and(z == 3, q % 2 == 1))

    def hears_above(q):
        return jnp.logical_or(inner, jnp.logical_and(z == 0, q // 2 == 0))

    def go_up(q):
        @pl.when(hears_below(q))
        def _():
            up_copy(q).wait_recv()

        @pl.when(z == 0)
        def _():
            upward[q] = diff[q]

        @pl.when(jnp.logical_and(z > 0, sends_up(q)))
        def _():
            upward[q] = diff[q] + below[q]

        @pl.when(sends_up(q))
        def _():
            up_copy(q).start()

    def go_down(q):
        @pl.when(hears_above(q))
        def _():
            down_copy(q).wait_recv()

        @pl.when(z == 3)
        def _():
            downward[q] = diff[q]

        @pl.when(jnp.logical_and(z < 3, sends_down(q)))
        def _():
            downward[q] = diff[q] + above[q]

        @pl.when(sends_down(q))
        def _():
            down_copy(q).start()

    def near(q):
        @pl.when(z < 2)
        def _():
            go_up(q)

        @pl.when(z >= 2)
        def _():
            go_down(q)

    def far(q):
        @pl.when(z < 2)
        def _():
            go_down(q)

        @pl.when(z >= 2)
        def _():
            go_up(q)

    early = [jnp.where(y == 0, t * 2 + x, x * 2 + t) for t in range(2)]
    late = [jnp.where(y == 0, t * 2 + 1 - x, (1 - x) * 2 + t) for t in range(2)]
    pair_copy(1).wait_recv()
    pair_copy(2).wait_recv()
    antisym(early[0])
    near(early[0])
    antisym(early[1])
    near(early[1])

    @pl.when(inner)
    def _():
        far(early[0])

    pair_copy(0).wait_recv()
    antisym(late[0])
    near(late[0])

    @pl.when(inner)
    def _():
        far(early[1])

    antisym(late[1])
    near(late[1])

    @pl.when(jnp.logical_not(inner))
    def _():
        far(early[0])
        far(early[1])

    far(late[0])
    far(late[1])

    def total_of(t, i):
        q = jnp.where(z < 2, z * 2 + t, t * 2 + z - 2)
        at = pl.ds(pl.multiple_of(i * h * h, 8), h * h)
        low = jnp.where(z > 0, below[q, at, :], jnp.float32(0.0))
        high = jnp.where(z < 3, above[q, at, :], jnp.float32(0.0))
        return diff[q, at, :] + low + high

    mine = jnp.where(z < 2, c, 0)
    for t in range(2):
        other[t] = total_of(t, jnp.where(z < 2, 1 - c, 1))
    last = pltpu.make_async_remote_copy(
        src_ref=other, dst_ref=kept.at[1], send_sem=last_send, recv_sem=last_recv,
        device_id={"virt": mate}, device_id_type=MESH,
    )
    last.start()
    for t in range(2):
        kept[0, t] = total_of(t, mine)

    def put(s):
        for t in range(2):

            @pl.loop(0, h)
            def _(a):
                at = pl.multiple_of((a * 4 + 2 * t + s) * h, 8)
                plain = kept[s, t, pl.ds(pl.multiple_of(a * h, 8), h), :]
                turned = kept[s, t, pl.ds(a, h, stride=h), :]
                out_ref[pl.ds(at, h), :] = jnp.where(z < 2, plain, -turned)

    put(0)
    last.wait_recv()
    put(1)

    last.wait_send()
    for d in range(2):
        amp_copy(d, 0).wait_send()
        amp_copy(d, 1).wait_send()
        pass_on(d).wait_send()
    for n in range(4):
        for i in range(2):
            core_copy(n, i).wait_send()
    for n in range(3):
        pair_copy(n).wait_send()
    for q in range(4):

        @pl.when(sends_up(q))
        def _():
            up_copy(q).wait_send()

        @pl.when(sends_down(q))
        def _():
            down_copy(q).wait_send()


def ladder_of(amplitudes, integrals, tile_width):
    h = tile_width // 4
    quad = 2 * h * h
    count, depth = amplitudes.shape
    owned = integrals.shape[0]
    step = owned // 8
    f32 = jnp.float32
    bf16 = jnp.bfloat16
    dma = pltpu.SemaphoreType.DMA
    return pl.pallas_call(
        functools.partial(ladder_kernel, h),
        out_shape=jax.ShapeDtypeStruct((tile_width * h, LANES), f32),
        in_specs=[pl.BlockSpec(memory_space=pltpu.VMEM), pl.BlockSpec(memory_space=pl.ANY)],
        out_specs=pl.BlockSpec(memory_space=pltpu.VMEM),
        scratch_shapes=[
            pltpu.VMEM((2, step, depth), f32),
            pltpu.VMEM((owned, depth), bf16),
            pltpu.VMEM((owned, depth), bf16),
            pltpu.VMEM((3, count, depth), f32),
            pltpu.VMEM((8 * LANES, depth), bf16),
            pltpu.VMEM((2, h, 2, 2, h, 4 * LANES), f32),
            pltpu.VMEM((4, 2, h, 2, h, LANES), f32),
            pltpu.VMEM((3, 2 * quad, LANES), f32),
            pltpu.VMEM((8 * quad, LANES), f32),
            pltpu.VMEM((4, quad, LANES), f32),
            pltpu.VMEM((4, quad, LANES), f32),
            pltpu.VMEM((4, quad, LANES), f32),
            pltpu.VMEM((4, quad, LANES), f32),
            pltpu.VMEM((4, quad, LANES), f32),
            pltpu.VMEM((2, 2, h * h, LANES), f32),
            pltpu.VMEM((2, h * h, LANES), f32),
            dma((2,)), dma((3, 2)), dma((3, 2)),
            dma((4, 2)), dma((4, 2)), dma((3,)), dma((3,)),
            dma((4,)), dma((4,)), dma((4,)), dma((4,)), dma, dma,
        ],
        compiler_params=pltpu.CompilerParams(
            collective_id=0, has_side_effects=True, vmem_limit_bytes=60 * 1024 * 1024
        ),
        name="ladder",
    )(amplitudes, integrals)


def block_body(amplitudes, integrals, eps_occ, eps_vir, pair_list):
    tile_width = eps_vir.shape[0] // 2
    count = amplitudes.shape[0]
    ladder = ladder_of(amplitudes, integrals, tile_width).T[:count]
    return (ladder, updated(ladder, eps_occ, eps_vir, pair_list))


def solution(mesh):
    in_specs = (P("pair", "virt"), P("pair", "virt"), P(), P(), P("pair", None))
    out_specs = (P("pair", "virt"), P("pair", "virt"))
    fits = mesh.shape["pair"] == 4 and mesh.shape["virt"] == 8

    def body(amplitudes, integrals, eps_occ, eps_vir, pair_list):
        tiled = eps_vir.shape[0] % 64 == 0 and amplitudes.shape[0] <= LANES
        chosen = block_body if fits and tiled else any_mesh_body
        return chosen(amplitudes, integrals, eps_occ, eps_vir, pair_list)

    return jax.shard_map(body, mesh=mesh, in_specs=in_specs, out_specs=out_specs, check_vma=False)
```

```python
import functools

import jax
import jax.numpy as jnp
from jax import lax
from jax.experimental import pallas as pl
from jax.experimental.pallas import tpu as pltpu
from jax.sharding import PartitionSpec as P

MESH = pl.DeviceIdType.MESH
LANES = 128


def antisymmetrize(partial_value, tile_width):
    blocks = partial_value.reshape(partial_value.shape[0], 2, tile_width, tile_width)
    mirrored = jnp.swapaxes(blocks[:, ::-1], 2, 3)
    return (blocks - mirrored).reshape(partial_value.shape)


def pair_energies(eps_occ, pair_list):
    occ_ids = lax.broadcasted_iota(jnp.int32, (1, 1, eps_occ.shape[0]), 2)
    one_hot = pair_list[:, :, None] == occ_ids
    return jnp.sum(jnp.where(one_hot, eps_occ[None, None, :], jnp.float32(0.0)), axis=(1, 2))


def sum_to_owners(antisym):
    return lax.psum_scatter(antisym, "virt", scatter_dimension=1, tiled=True)


def updated(ladder, eps_occ, eps_vir, pair_list):
    tile_width = eps_vir.shape[0] // 2
    column_count = ladder.shape[1]
    energy_tiles = eps_vir.reshape(2, tile_width)
    virt_energy = (energy_tiles[:, :, None] + energy_tiles[::-1][:, None, :]).reshape(
        2 * tile_width * tile_width
    )
    local_energy = lax.dynamic_slice_in_dim(
        virt_energy, lax.axis_index("virt") * column_count, column_count
    )
    pair_energy = pair_energies(eps_occ, pair_list)
    return ladder / (pair_energy[:, None] - local_energy[None, :])


def any_mesh_body(amplitudes, integrals, eps_occ, eps_vir, pair_list):
    tile_width = eps_vir.shape[0] // 2
    by_pairs = lax.dot_general(
        lax.all_gather(amplitudes, "pair", axis=0, tiled=True),
        integrals,
        (((1,), (1,)), ((), ())),
        precision=lax.Precision.HIGHEST,
        preferred_element_type=jnp.float32,
    )
    partial_value = lax.all_to_all(by_pairs, "pair", split_axis=0, concat_axis=1, tiled=True)
    ladder = sum_to_owners(antisymmetrize(partial_value, tile_width))
    return (ladder, updated(ladder, eps_occ, eps_vir, pair_list))


def split(value):
    high = value.astype(jnp.bfloat16)
    return high, (value - high.astype(jnp.float32)).astype(jnp.bfloat16)


def times(left, right):
    return lax.dot_general(
        left, right, (((1,), (1,)), ((), ())), preferred_element_type=jnp.float32
    )


def ladder_kernel(
    h, amp_ref, int_ref, out_ref, stage, int_high, int_low, blocks, weights, ct_ref,
    got, summed, rows, diff, below, above, upward, downward, kept, other, placed,
    stage_sem, amp_send, amp_recv,
    core_send, core_recv, pair_send, pair_recv, up_send, up_recv, down_send, down_recv,
    last_send, last_recv,
):
    r = lax.axis_index("pair")
    v = lax.axis_index("virt")
    z = v // 2
    c = v % 2
    mate = v + 1 - 2 * c
    x = r % 2
    y = r // 2
    peers = (y * 2 + (1 - x), (1 - y) * 2 + x, (1 - y) * 2 + (1 - x))
    count, depth = amp_ref.shape
    cut = count // 16 * 8
    parts = (pl.ds(0, cut), pl.ds(cut, count - cut))
    step = stage.shape[1]
    steps = int_ref.shape[0] // step

    def stage_copy(t):
        return pltpu.make_async_copy(
            int_ref.at[pl.ds(pl.multiple_of(t * step, 8), step)],
            stage.at[t % 2],
            stage_sem.at[t % 2],
        )

    stage_copy(0).start()
    stage_copy(1).start()

    barrier = pltpu.get_barrier_semaphore()
    pl.semaphore_signal(barrier, inc=1, device_id={"virt": mate}, device_id_type=MESH)
    for peer in peers:
        pl.semaphore_signal(barrier, inc=1, device_id={"pair": peer}, device_id_type=MESH)

    @pl.when(z < 3)
    def _():
        pl.semaphore_signal(barrier, inc=1, device_id={"virt": v + 2}, device_id_type=MESH)

    @pl.when(z > 0)
    def _():
        pl.semaphore_signal(barrier, inc=1, device_id={"virt": v - 2}, device_id_type=MESH)

    inner = jnp.logical_and(z > 0, z < 3)

    @pl.when(inner)
    def _():
        pl.semaphore_wait(barrier, 6)

    @pl.when(jnp.logical_not(inner))
    def _():
        pl.semaphore_wait(barrier, 5)

    def amp_copy(d, part):
        return pltpu.make_async_remote_copy(
            src_ref=amp_ref.at[parts[part]],
            dst_ref=blocks.at[d, parts[part]],
            send_sem=amp_send.at[d, part],
            recv_sem=amp_recv.at[d, part],
            device_id={"pair": peers[d]},
            device_id_type=MESH,
        )

    def pass_on(d):
        return pltpu.make_async_remote_copy(
            src_ref=blocks.at[d, parts[d]],
            dst_ref=blocks.at[2, parts[d]],
            send_sem=amp_send.at[2, d],
            recv_sem=amp_recv.at[2, d],
            device_id={"pair": peers[1 - d]},
            device_id_type=MESH,
        )

    for late in range(2):
        for d in range(2):
            amp_copy(d, d if late == 0 else 1 - d).start()

    def weigh(source, high_at, low_at):
        wide = 2 * LANES

        @pl.loop(0, depth // wide)
        def _(k):
            columns = pl.ds(pl.multiple_of(k * wide, wide), wide)
            value = source[:, columns]
            if count < LANES:
                value = jnp.concatenate(
                    [value, jnp.zeros((LANES - count, wide), jnp.float32)], axis=0
                )
            high, low = split(value)
            weights[pl.ds(high_at * LANES, LANES), columns] = high
            weights[pl.ds(low_at * LANES, LANES), columns] = low

    def keep(t, size, lanes, value):
        per = size // (4 * h)
        i = t // (h // per)
        at = pl.multiple_of(t % (h // per) * per, per)
        ct_ref[i, pl.ds(at, per), :, :, :, lanes] = value.reshape(per, 2, 2, h, value.shape[1])

    def one_block(high, low, at):
        both = times(high, weights[pl.ds(at * LANES, 2 * LANES), :])
        rest = times(low, weights[pl.ds(at * LANES, LANES), :])
        return both[:, :LANES] + both[:, LANES:] + rest

    weigh(amp_ref, 0, 1)

    @pl.loop(0, steps)
    def _(t):
        stage_copy(t).wait()
        high, low = split(stage[t % 2])
        at = pl.ds(pl.multiple_of(t * step, 16), step)
        int_high[at, :] = high
        int_low[at, :] = low

        @pl.when(t + 2 < steps)
        def _():
            stage_copy(t + 2).start()

        keep(t, step, pl.ds(3 * LANES, LANES), one_block(int_high[at, :], int_low[at, :], 0))

    for d in range(2):
        amp_copy(d, d).wait_recv()
        pass_on(d).start()

    order = (peers[2], peers[0], peers[1], r)

    def core_copy(n, i):
        return pltpu.make_async_remote_copy(
            src_ref=ct_ref.at[i, :, :, (1 - c + i) % 2, :, pl.ds(n * LANES, LANES)],
            dst_ref=got.at[n, i],
            send_sem=core_send.at[n, i],
            recv_sem=core_recv.at[n, i],
            device_id={"virt": mate},
            device_id_type=MESH,
        )

    def pair_copy(n, piece):
        bh = jnp.where(piece == 0, 1 - x, x) if n == 1 else piece
        return pltpu.make_async_remote_copy(
            src_ref=summed.at[n, :, bh],
            dst_ref=rows.at[r, :, bh],
            send_sem=pair_send.at[n, piece],
            recv_sem=pair_recv.at[n, piece],
            device_id={"pair": order[n]},
            device_id_type=MESH,
        )

    def pair_arrived(n, piece):
        pair_copy(n, piece).wait_recv()

    def core_start(n):
        for i in range(2):
            core_copy(n, i).start()

    def core_add(n):
        lanes = pl.ds(n * LANES, LANES)
        for i in range(2):
            core_copy(n, i).wait_recv()

            @pl.loop(0, h, unroll=4)
            def _(a):
                for bh in range(2):
                    total = ct_ref[i, a, bh, (c + i) % 2, :, lanes] + got[n, i, a, bh]
                    if n < 3:
                        summed[n, i * h + a, bh] = total
                    else:
                        rows[r, i * h + a, bh] = total

    core_start(3)
    for d in range(2):
        amp_copy(d, 1 - d).wait_recv()
        weigh(blocks.at[d], 4 + d, 6 + d)
    big = 2 * step

    @pl.loop(0, steps // 2)
    def _(t):
        at = pl.ds(pl.multiple_of(t * big, 16), big)
        near_high = weights[pl.ds(4 * LANES, 2 * LANES), :]
        near_low = weights[pl.ds(6 * LANES, 2 * LANES), :]
        value = times(int_high[at, :], near_high) + times(int_high[at, :], near_low)
        value = value + times(int_low[at, :], near_high)
        keep(t, big, pl.ds(LANES, 2 * LANES), value)

    core_start(1)
    core_start(2)
    core_add(3)
    core_add(1)
    pair_copy(1, 0).start()
    core_add(2)
    pair_copy(2, 0).start()
    pair_copy(2, 1).start()
    pair_copy(1, 1).start()
    for d in range(2):
        pass_on(d).wait_recv()
    weigh(blocks.at[2], 2, 3)

    @pl.loop(0, steps // 2)
    def _(t):
        at = pl.ds(pl.multiple_of(t * big, 16), big)
        keep(t, big, pl.ds(0, LANES), one_block(int_high[at, :], int_low[at, :], 2))

    core_start(0)
    core_add(0)
    pair_copy(0, 0).start()
    pair_copy(0, 1).start()

    def antisym(q, i):
        ah = q // 2
        bh = q % 2
        mirror = (c + i) % 2

        @pl.loop(0, h, unroll=4)
        def _(a):
            plain = rows[ah, i * h + a, bh]
            turned = rows[2 + bh, pl.ds(mirror * h, h), ah, a, :]
            diff[q * 2 + i, pl.ds(pl.multiple_of(a * h, 8), h), :] = plain - turned

    def up_copy(q):
        return pltpu.make_async_remote_copy(
            src_ref=upward.at[q], dst_ref=below.at[q],
            send_sem=up_send.at[q], recv_sem=up_recv.at[q],
            device_id={"virt": v + 2}, device_id_type=MESH,
        )

    def down_copy(q):
        return pltpu.make_async_remote_copy(
            src_ref=downward.at[q], dst_ref=above.at[q],
            send_sem=down_send.at[q], recv_sem=down_recv.at[q],
            device_id={"virt": v - 2}, device_id_type=MESH,
        )

    def sends_up(q):
        return jnp.logical_or(z < 2, jnp.logical_and(z == 2, q // 2 % 2 == 1))

    def sends_down(q):
        return jnp.logical_or(z > 1, jnp.logical_and(z == 1, q // 4 == 0))

    def hears_below(q):
        return jnp.logical_or(inner, jnp.logical_and(z == 3, q // 2 % 2 == 1))

    def hears_above(q):
        return jnp.logical_or(inner, jnp.logical_and(z == 0, q // 4 == 0))

    def go_up(q):
        @pl.when(hears_below(q))
        def _():
            up_copy(q).wait_recv()

        @pl.when(z == 0)
        def _():
            upward[q] = diff[q]

        @pl.when(jnp.logical_and(z > 0, sends_up(q)))
        def _():
            upward[q] = diff[q] + below[q]

        @pl.when(sends_up(q))
        def _():
            up_copy(q).start()

    def go_down(q):
        @pl.when(hears_above(q))
        def _():
            down_copy(q).wait_recv()

        @pl.when(z == 3)
        def _():
            downward[q] = diff[q]

        @pl.when(jnp.logical_and(z < 3, sends_down(q)))
        def _():
            downward[q] = diff[q] + above[q]

        @pl.when(sends_down(q))
        def _():
            down_copy(q).start()

    def near(q):
        @pl.when(z < 2)
        def _():
            go_up(q)

        @pl.when(z >= 2)
        def _():
            go_down(q)

    def far(q):
        @pl.when(z < 2)
        def _():
            go_down(q)

        @pl.when(z >= 2)
        def _():
            go_up(q)

    early = [jnp.where(y == 0, t * 2 + x, x * 2 + t) for t in range(2)]
    late = [jnp.where(y == 0, t * 2 + 1 - x, (1 - x) * 2 + t) for t in range(2)]
    quads = early + late
    chunks = [q * 2 + i for q in quads for i in range(2)]
    needs = (((1, 0), (2, 0)), ((2, 1),), ((1, 1), (0, 0)), ((0, 1),))
    lag = 2
    for s in range(8):
        if s % 2 == 0:
            for n, piece in needs[s // 2]:
                pair_arrived(n, piece)
        antisym(quads[s // 2], s % 2)
        near(chunks[s])
        if s >= lag:

            @pl.when(inner)
            def _():
                far(chunks[s - lag])

    @pl.when(jnp.logical_not(inner))
    def _():
        for s in range(8 - lag):
            far(chunks[s])

    for s in range(8 - lag, 8):
        far(chunks[s])

    def total_of(t, i):
        q = jnp.where(z < 2, z * 2 + t, t * 2 + z - 2) * 2 + i
        low = jnp.where(z > 0, below[q], jnp.float32(0.0))
        high = jnp.where(z < 3, above[q], jnp.float32(0.0))
        return diff[q] + low + high

    mine = jnp.where(z < 2, c, 0)
    for t in range(2):
        other[t] = total_of(t, jnp.where(z < 2, 1 - c, 1))
    last = pltpu.make_async_remote_copy(
        src_ref=other, dst_ref=kept.at[1], send_sem=last_send, recv_sem=last_recv,
        device_id={"virt": mate}, device_id_type=MESH,
    )
    last.start()
    for t in range(2):
        kept[0, t] = total_of(t, mine)

    def put(s):
        for t in range(2):

            @pl.loop(0, h, unroll=4)
            def _(a):
                at = pl.multiple_of((a * 4 + 2 * t + s) * h, 8)
                plain = kept[s, t, pl.ds(pl.multiple_of(a * h, 8), h), :]
                turned = kept[s, t, pl.ds(a, h, stride=h), :]
                placed[pl.ds(at, h), :] = jnp.where(z < 2, plain, -turned)

    put(0)
    last.wait_recv()
    put(1)

    for n in range(out_ref.shape[1] // LANES):
        at = pl.ds(n * LANES, LANES)
        out_ref[:, at] = placed[at, :].T[:count]

    last.wait_send()
    for d in range(2):
        amp_copy(d, 0).wait_send()
        amp_copy(d, 1).wait_send()
        pass_on(d).wait_send()
    for n in range(4):
        for i in range(2):
            core_copy(n, i).wait_send()
    for n in range(3):
        for piece in range(2):
            pair_copy(n, piece).wait_send()
    for q in range(8):

        @pl.when(sends_up(q))
        def _():
            up_copy(q).wait_send()

        @pl.when(sends_down(q))
        def _():
            down_copy(q).wait_send()


def ladder_of(amplitudes, integrals, tile_width):
    h = tile_width // 4
    count, depth = amplitudes.shape
    owned = integrals.shape[0]
    step = owned // 8
    f32 = jnp.float32
    bf16 = jnp.bfloat16
    dma = pltpu.SemaphoreType.DMA
    return pl.pallas_call(
        functools.partial(ladder_kernel, h),
        out_shape=jax.ShapeDtypeStruct((count, tile_width * h), f32),
        in_specs=[pl.BlockSpec(memory_space=pltpu.VMEM), pl.BlockSpec(memory_space=pl.ANY)],
        out_specs=pl.BlockSpec(memory_space=pltpu.VMEM),
        scratch_shapes=[
            pltpu.VMEM((2, step, depth), f32),
            pltpu.VMEM((owned, depth), bf16),
            pltpu.VMEM((owned, depth), bf16),
            pltpu.VMEM((3, count, depth), f32),
            pltpu.VMEM((8 * LANES, depth), bf16),
            pltpu.VMEM((2, h, 2, 2, h, 4 * LANES), f32),
            pltpu.VMEM((4, 2, h, 2, h, LANES), f32),
            pltpu.VMEM((3, 2 * h, 2, h, LANES), f32),
            pltpu.VMEM((4, 2 * h, 2, h, LANES), f32),
            pltpu.VMEM((8, h * h, LANES), f32),
            pltpu.VMEM((8, h * h, LANES), f32),
            pltpu.VMEM((8, h * h, LANES), f32),
            pltpu.VMEM((8, h * h, LANES), f32),
            pltpu.VMEM((8, h * h, LANES), f32),
            pltpu.VMEM((2, 2, h * h, LANES), f32),
            pltpu.VMEM((2, h * h, LANES), f32),
            pltpu.VMEM((tile_width * h, LANES), f32),
            dma((2,)), dma((3, 2)), dma((3, 2)),
            dma((4, 2)), dma((4, 2)), dma((3, 2)), dma((3, 2)),
            dma((8,)), dma((8,)), dma((8,)), dma((8,)), dma, dma,
        ],
        compiler_params=pltpu.CompilerParams(
            collective_id=0, has_side_effects=True, vmem_limit_bytes=60 * 1024 * 1024
        ),
        name="ladder",
    )(amplitudes, integrals)


def block_body(amplitudes, integrals, eps_occ, eps_vir, pair_list):
    tile_width = eps_vir.shape[0] // 2
    ladder = ladder_of(amplitudes, integrals, tile_width)
    return (ladder, updated(ladder, eps_occ, eps_vir, pair_list))


def solution(mesh):
    in_specs = (P("pair", "virt"), P("pair", "virt"), P(), P(), P("pair", None))
    out_specs = (P("pair", "virt"), P("pair", "virt"))
    fits = mesh.shape["pair"] == 4 and mesh.shape["virt"] == 8

    def body(amplitudes, integrals, eps_occ, eps_vir, pair_list):
        tiled = eps_vir.shape[0] % 64 == 0 and amplitudes.shape[0] <= LANES
        chosen = block_body if fits and tiled else any_mesh_body
        return chosen(amplitudes, integrals, eps_occ, eps_vir, pair_list)

    return jax.shard_map(body, mesh=mesh, in_specs=in_specs, out_specs=out_specs, check_vma=False)
```

```python
import functools

import jax
import jax.numpy as jnp
from jax import lax
from jax.experimental import pallas as pl
from jax.experimental.pallas import tpu as pltpu
from jax.sharding import PartitionSpec as P

MESH = pl.DeviceIdType.MESH
LANES = 128


def antisymmetrize(partial_value, tile_width):
    blocks = partial_value.reshape(partial_value.shape[0], 2, tile_width, tile_width)
    mirrored = jnp.swapaxes(blocks[:, ::-1], 2, 3)
    return (blocks - mirrored).reshape(partial_value.shape)


def pair_energies(eps_occ, pair_list):
    occ_ids = lax.broadcasted_iota(jnp.int32, (1, 1, eps_occ.shape[0]), 2)
    one_hot = pair_list[:, :, None] == occ_ids
    return jnp.sum(jnp.where(one_hot, eps_occ[None, None, :], jnp.float32(0.0)), axis=(1, 2))


def sum_to_owners(antisym):
    return lax.psum_scatter(antisym, "virt", scatter_dimension=1, tiled=True)


def updated(ladder, eps_occ, eps_vir, pair_list):
    tile_width = eps_vir.shape[0] // 2
    column_count = ladder.shape[1]
    energy_tiles = eps_vir.reshape(2, tile_width)
    virt_energy = (energy_tiles[:, :, None] + energy_tiles[::-1][:, None, :]).reshape(
        2 * tile_width * tile_width
    )
    local_energy = lax.dynamic_slice_in_dim(
        virt_energy, lax.axis_index("virt") * column_count, column_count
    )
    pair_energy = pair_energies(eps_occ, pair_list)
    return ladder / (pair_energy[:, None] - local_energy[None, :])


def any_mesh_body(amplitudes, integrals, eps_occ, eps_vir, pair_list):
    tile_width = eps_vir.shape[0] // 2
    by_pairs = lax.dot_general(
        lax.all_gather(amplitudes, "pair", axis=0, tiled=True),
        integrals,
        (((1,), (1,)), ((), ())),
        precision=lax.Precision.HIGHEST,
        preferred_element_type=jnp.float32,
    )
    partial_value = lax.all_to_all(by_pairs, "pair", split_axis=0, concat_axis=1, tiled=True)
    ladder = sum_to_owners(antisymmetrize(partial_value, tile_width))
    return (ladder, updated(ladder, eps_occ, eps_vir, pair_list))


def split(value):
    high = value.astype(jnp.bfloat16)
    return high, (value - high.astype(jnp.float32)).astype(jnp.bfloat16)


def times(left, right):
    return lax.dot_general(
        left, right, (((1,), (1,)), ((), ())), preferred_element_type=jnp.float32
    )


def ladder_kernel(
    h, amp_ref, int_ref, out_ref, stage, int_high, int_low, blocks, weights, ct_ref,
    got, summed, rows, diff, below, above, upward, downward, kept, other, placed,
    stage_sem, amp_send, amp_recv,
    core_send, core_recv, pair_send, pair_recv, up_send, up_recv, down_send, down_recv,
    last_send, last_recv,
):
    r = lax.axis_index("pair")
    v = lax.axis_index("virt")
    z = v // 2
    c = v % 2
    mate = v + 1 - 2 * c
    x = r % 2
    y = r // 2
    peers = (y * 2 + (1 - x), (1 - y) * 2 + x, (1 - y) * 2 + (1 - x))
    count, depth = amp_ref.shape
    cut = count // 16 * 8
    parts = (pl.ds(0, cut), pl.ds(cut, count - cut))
    step = stage.shape[1]
    steps = int_ref.shape[0] // step

    def stage_copy(t):
        return pltpu.make_async_copy(
            int_ref.at[pl.ds(pl.multiple_of(t * step, 8), step)],
            stage.at[t % 2],
            stage_sem.at[t % 2],
        )

    stage_copy(0).start()
    stage_copy(1).start()

    barrier = pltpu.get_barrier_semaphore()
    pl.semaphore_signal(barrier, inc=1, device_id={"virt": mate}, device_id_type=MESH)
    for peer in peers:
        pl.semaphore_signal(barrier, inc=1, device_id={"pair": peer}, device_id_type=MESH)

    @pl.when(z < 3)
    def _():
        pl.semaphore_signal(barrier, inc=1, device_id={"virt": v + 2}, device_id_type=MESH)

    @pl.when(z > 0)
    def _():
        pl.semaphore_signal(barrier, inc=1, device_id={"virt": v - 2}, device_id_type=MESH)

    inner = jnp.logical_and(z > 0, z < 3)

    @pl.when(inner)
    def _():
        pl.semaphore_wait(barrier, 6)

    @pl.when(jnp.logical_not(inner))
    def _():
        pl.semaphore_wait(barrier, 5)

    def amp_copy(d, part):
        return pltpu.make_async_remote_copy(
            src_ref=amp_ref.at[parts[part]],
            dst_ref=blocks.at[d, parts[part]],
            send_sem=amp_send.at[d, part],
            recv_sem=amp_recv.at[d, part],
            device_id={"pair": peers[d]},
            device_id_type=MESH,
        )

    def pass_on(d):
        return pltpu.make_async_remote_copy(
            src_ref=blocks.at[d, parts[d]],
            dst_ref=blocks.at[2, parts[d]],
            send_sem=amp_send.at[2, d],
            recv_sem=amp_recv.at[2, d],
            device_id={"pair": peers[1 - d]},
            device_id_type=MESH,
        )

    for late in range(2):
        for d in range(2):
            amp_copy(d, d if late == 0 else 1 - d).start()

    def weigh(source, high_at, low_at):
        wide = 2 * LANES

        @pl.loop(0, depth // wide)
        def _(k):
            columns = pl.ds(pl.multiple_of(k * wide, wide), wide)
            value = source[:, columns]
            if count < LANES:
                value = jnp.concatenate(
                    [value, jnp.zeros((LANES - count, wide), jnp.float32)], axis=0
                )
            high, low = split(value)
            weights[pl.ds(high_at * LANES, LANES), columns] = high
            weights[pl.ds(low_at * LANES, LANES), columns] = low

    def keep(t, size, lanes, value):
        per = size // (4 * h)
        i = t // (h // per)
        at = pl.multiple_of(t % (h // per) * per, per)
        ct_ref[i, pl.ds(at, per), :, :, :, lanes] = value.reshape(per, 2, 2, h, value.shape[1])

    def one_block(high, low, at):
        both = times(high, weights[pl.ds(at * LANES, 2 * LANES), :])
        rest = times(low, weights[pl.ds(at * LANES, LANES), :])
        return both[:, :LANES] + both[:, LANES:] + rest

    weigh(amp_ref, 0, 1)

    @pl.loop(0, steps)
    def _(t):
        stage_copy(t).wait()
        high, low = split(stage[t % 2])
        at = pl.ds(pl.multiple_of(t * step, 16), step)
        int_high[at, :] = high
        int_low[at, :] = low

        @pl.when(t + 2 < steps)
        def _():
            stage_copy(t + 2).start()

        keep(t, step, pl.ds(3 * LANES, LANES), one_block(int_high[at, :], int_low[at, :], 0))

    for d in range(2):
        amp_copy(d, d).wait_recv()
        pass_on(d).start()

    order = (peers[2], peers[0], peers[1], r)

    def core_copy(n, i):
        return pltpu.make_async_remote_copy(
            src_ref=ct_ref.at[i, :, :, (1 - c + i) % 2, :, pl.ds(n * LANES, LANES)],
            dst_ref=got.at[n, i],
            send_sem=core_send.at[n, i],
            recv_sem=core_recv.at[n, i],
            device_id={"virt": mate},
            device_id_type=MESH,
        )

    def pair_copy(n, piece):
        bh = jnp.where(piece == 0, 1 - x, x) if n == 1 else piece
        return pltpu.make_async_remote_copy(
            src_ref=summed.at[n, :, bh],
            dst_ref=rows.at[r, :, bh],
            send_sem=pair_send.at[n, piece],
            recv_sem=pair_recv.at[n, piece],
            device_id={"pair": order[n]},
            device_id_type=MESH,
        )

    def pair_arrived(n, piece):
        pair_copy(n, piece).wait_recv()

    def core_start(n):
        for i in range(2):
            core_copy(n, i).start()

    half = steps // 4

    def core_add(n):
        lanes = pl.ds(n * LANES, LANES)
        for i in range(2):
            core_copy(n, i).wait_recv()

            @pl.loop(0, h, unroll=4)
            def _(a):
                for bh in range(2):
                    total = ct_ref[i, a, bh, (c + i) % 2, :, lanes] + got[n, i, a, bh]
                    if n < 3:
                        summed[n, i * h + a, bh] = total
                    else:
                        rows[r, i * h + a, bh] = total

    core_start(3)
    for d in range(2):
        amp_copy(d, 1 - d).wait_recv()
        weigh(blocks.at[d], 4 + d, 6 + d)
    big = 2 * step

    for i in range(2):

        @pl.loop(i * half, (i + 1) * half)
        def _(t):
            at = pl.ds(pl.multiple_of(t * big, 16), big)
            near_high = weights[pl.ds(4 * LANES, 2 * LANES), :]
            near_low = weights[pl.ds(6 * LANES, 2 * LANES), :]
            value = times(int_high[at, :], near_high) + times(int_high[at, :], near_low)
            value = value + times(int_low[at, :], near_high)
            keep(t, big, pl.ds(LANES, 2 * LANES), value)

        core_copy(1, i).start()
        core_copy(2, i).start()

    core_add(1)
    pair_copy(1, 0).start()
    core_add(2)
    pair_copy(2, 0).start()
    pair_copy(2, 1).start()
    pair_copy(1, 1).start()
    core_add(3)
    for d in range(2):
        pass_on(d).wait_recv()
    weigh(blocks.at[2], 2, 3)

    @pl.loop(0, steps // 2)
    def _(t):
        at = pl.ds(pl.multiple_of(t * big, 16), big)
        keep(t, big, pl.ds(0, LANES), one_block(int_high[at, :], int_low[at, :], 2))

    core_start(0)
    core_add(0)
    pair_copy(0, 0).start()
    pair_copy(0, 1).start()

    def antisym(q, i, u):
        ah = q // 2
        bh = q % 2
        mirror = (c + i) % 2

        @pl.loop(0, h // 2, unroll=4)
        def _(n):
            a = u * (h // 2) + n
            plain = rows[ah, i * h + a, bh]
            turned = rows[2 + bh, pl.ds(mirror * h, h), ah, a, :]
            diff[q * 4 + i * 2 + u, pl.ds(pl.multiple_of(n * h, 8), h), :] = plain - turned

    def up_copy(q):
        return pltpu.make_async_remote_copy(
            src_ref=upward.at[q], dst_ref=below.at[q],
            send_sem=up_send.at[q], recv_sem=up_recv.at[q],
            device_id={"virt": v + 2}, device_id_type=MESH,
        )

    def down_copy(q):
        return pltpu.make_async_remote_copy(
            src_ref=downward.at[q], dst_ref=above.at[q],
            send_sem=down_send.at[q], recv_sem=down_recv.at[q],
            device_id={"virt": v - 2}, device_id_type=MESH,
        )

    def sends_up(q):
        return jnp.logical_or(z < 2, jnp.logical_and(z == 2, q // 4 % 2 == 1))

    def sends_down(q):
        return jnp.logical_or(z > 1, jnp.logical_and(z == 1, q // 8 == 0))

    def hears_below(q):
        return jnp.logical_or(inner, jnp.logical_and(z == 3, q // 4 % 2 == 1))

    def hears_above(q):
        return jnp.logical_or(inner, jnp.logical_and(z == 0, q // 8 == 0))

    def go_up(q):
        @pl.when(hears_below(q))
        def _():
            up_copy(q).wait_recv()

        @pl.when(z == 0)
        def _():
            upward[q] = diff[q]

        @pl.when(jnp.logical_and(z > 0, sends_up(q)))
        def _():
            upward[q] = diff[q] + below[q]

        @pl.when(sends_up(q))
        def _():
            up_copy(q).start()

    def go_down(q):
        @pl.when(hears_above(q))
        def _():
            down_copy(q).wait_recv()

        @pl.when(z == 3)
        def _():
            downward[q] = diff[q]

        @pl.when(jnp.logical_and(z < 3, sends_down(q)))
        def _():
            downward[q] = diff[q] + above[q]

        @pl.when(sends_down(q))
        def _():
            down_copy(q).start()

    def near(q):
        @pl.when(z < 2)
        def _():
            go_up(q)

        @pl.when(z >= 2)
        def _():
            go_down(q)

    def far(q):
        @pl.when(z < 2)
        def _():
            go_down(q)

        @pl.when(z >= 2)
        def _():
            go_up(q)

    early = [jnp.where(y == 0, t * 2 + x, x * 2 + t) for t in range(2)]
    late = [jnp.where(y == 0, t * 2 + 1 - x, (1 - x) * 2 + t) for t in range(2)]
    quads = early + late
    chunks = [q * 4 + n for q in quads for n in range(4)]
    needs = (((1, 0), (2, 0)), ((2, 1),), ((1, 1), (0, 0)), ((0, 1),))
    lag = 3
    for s in range(16):
        if s % 4 == 0:
            for n, piece in needs[s // 4]:
                pair_arrived(n, piece)
        antisym(quads[s // 4], s // 2 % 2, s % 2)
        near(chunks[s])
        if s >= lag:

            @pl.when(inner)
            def _():
                far(chunks[s - lag])

    @pl.when(jnp.logical_not(inner))
    def _():
        for s in range(16 - lag):
            far(chunks[s])

    for s in range(16 - lag, 16):
        far(chunks[s])

    def total_of(t, i):
        q = pl.ds(jnp.where(z < 2, z * 2 + t, t * 2 + z - 2) * 4 + i * 2, 2)
        low = jnp.where(z > 0, below[q], jnp.float32(0.0))
        high = jnp.where(z < 3, above[q], jnp.float32(0.0))
        return (diff[q] + low + high).reshape(h * h, LANES)

    mine = jnp.where(z < 2, c, 0)
    for t in range(2):
        other[t] = total_of(t, jnp.where(z < 2, 1 - c, 1))
    last = pltpu.make_async_remote_copy(
        src_ref=other, dst_ref=kept.at[1], send_sem=last_send, recv_sem=last_recv,
        device_id={"virt": mate}, device_id_type=MESH,
    )
    last.start()
    for t in range(2):
        kept[0, t] = total_of(t, mine)

    def put(s):
        for t in range(2):

            @pl.loop(0, h, unroll=4)
            def _(a):
                at = pl.multiple_of((a * 4 + 2 * t + s) * h, 8)
                plain = kept[s, t, pl.ds(pl.multiple_of(a * h, 8), h), :]
                turned = kept[s, t, pl.ds(a, h, stride=h), :]
                placed[pl.ds(at, h), :] = jnp.where(z < 2, plain, turned)

    put(0)
    last.wait_recv()
    put(1)

    for n in range(out_ref.shape[1] // LANES):
        at = pl.ds(n * LANES, LANES)
        out_ref[:, at] = placed[at, :].T[:count]

    last.wait_send()
    for d in range(2):
        amp_copy(d, 0).wait_send()
        amp_copy(d, 1).wait_send()
        pass_on(d).wait_send()
    for n in range(4):
        for i in range(2):
            core_copy(n, i).wait_send()
    for n in range(3):
        for piece in range(2):
            pair_copy(n, piece).wait_send()
    for q in range(16):

        @pl.when(sends_up(q))
        def _():
            up_copy(q).wait_send()

        @pl.when(sends_down(q))
        def _():
            down_copy(q).wait_send()


def ladder_of(amplitudes, integrals, tile_width):
    h = tile_width // 4
    count, depth = amplitudes.shape
    owned = integrals.shape[0]
    step = owned // 8
    f32 = jnp.float32
    bf16 = jnp.bfloat16
    dma = pltpu.SemaphoreType.DMA
    return pl.pallas_call(
        functools.partial(ladder_kernel, h),
        out_shape=jax.ShapeDtypeStruct((count, tile_width * h), f32),
        in_specs=[pl.BlockSpec(memory_space=pltpu.VMEM), pl.BlockSpec(memory_space=pl.ANY)],
        out_specs=pl.BlockSpec(memory_space=pltpu.VMEM),
        scratch_shapes=[
            pltpu.VMEM((2, step, depth), f32),
            pltpu.VMEM((owned, depth), bf16),
            pltpu.VMEM((owned, depth), bf16),
            pltpu.VMEM((3, count, depth), f32),
            pltpu.VMEM((8 * LANES, depth), bf16),
            pltpu.VMEM((2, h, 2, 2, h, 4 * LANES), f32),
            pltpu.VMEM((4, 2, h, 2, h, LANES), f32),
            pltpu.VMEM((3, 2 * h, 2, h, LANES), f32),
            pltpu.VMEM((4, 2 * h, 2, h, LANES), f32),
            pltpu.VMEM((16, h * h // 2, LANES), f32),
            pltpu.VMEM((16, h * h // 2, LANES), f32),
            pltpu.VMEM((16, h * h // 2, LANES), f32),
            pltpu.VMEM((16, h * h // 2, LANES), f32),
            pltpu.VMEM((16, h * h // 2, LANES), f32),
            pltpu.VMEM((2, 2, h * h, LANES), f32),
            pltpu.VMEM((2, h * h, LANES), f32),
            pltpu.VMEM((tile_width * h, LANES), f32),
            dma((2,)), dma((3, 2)), dma((3, 2)),
            dma((4, 2)), dma((4, 2)), dma((3, 2)), dma((3, 2)),
            dma((16,)), dma((16,)), dma((16,)), dma((16,)), dma, dma,
        ],
        compiler_params=pltpu.CompilerParams(
            collective_id=0, has_side_effects=True, vmem_limit_bytes=60 * 1024 * 1024
        ),
        name="ladder",
    )(amplitudes, integrals)


def block_body(amplitudes, integrals, eps_occ, eps_vir, pair_list):
    tile_width = eps_vir.shape[0] // 2
    first = lax.axis_index("virt") < lax.axis_size("virt") // 2
    sign = jnp.where(first, jnp.float32(1.0), jnp.float32(-1.0))
    ladder = sign * ladder_of(amplitudes, integrals, tile_width)
    return (ladder, updated(ladder, eps_occ, eps_vir, pair_list))


def solution(mesh):
    in_specs = (P("pair", "virt"), P("pair", "virt"), P(), P(), P("pair", None))
    out_specs = (P("pair", "virt"), P("pair", "virt"))
    fits = mesh.shape["pair"] == 4 and mesh.shape["virt"] == 8

    def body(amplitudes, integrals, eps_occ, eps_vir, pair_list):
        tiled = eps_vir.shape[0] % 64 == 0 and amplitudes.shape[0] <= LANES
        chosen = block_body if fits and tiled else any_mesh_body
        return chosen(amplitudes, integrals, eps_occ, eps_vir, pair_list)

    return jax.shard_map(body, mesh=mesh, in_specs=in_specs, out_specs=out_specs, check_vma=False)
```

```python
import functools

import jax
import jax.numpy as jnp
from jax import lax
from jax.experimental import pallas as pl
from jax.experimental.pallas import tpu as pltpu
from jax.sharding import PartitionSpec as P

MESH = pl.DeviceIdType.MESH
LANES = 128


def antisymmetrize(partial_value, tile_width):
    blocks = partial_value.reshape(partial_value.shape[0], 2, tile_width, tile_width)
    mirrored = jnp.swapaxes(blocks[:, ::-1], 2, 3)
    return (blocks - mirrored).reshape(partial_value.shape)


def pair_energies(eps_occ, pair_list):
    occ_ids = lax.broadcasted_iota(jnp.int32, (1, 1, eps_occ.shape[0]), 2)
    one_hot = pair_list[:, :, None] == occ_ids
    return jnp.sum(jnp.where(one_hot, eps_occ[None, None, :], jnp.float32(0.0)), axis=(1, 2))


def sum_to_owners(antisym):
    return lax.psum_scatter(antisym, "virt", scatter_dimension=1, tiled=True)


def updated(ladder, eps_occ, eps_vir, pair_list):
    tile_width = eps_vir.shape[0] // 2
    column_count = ladder.shape[1]
    energy_tiles = eps_vir.reshape(2, tile_width)
    virt_energy = (energy_tiles[:, :, None] + energy_tiles[::-1][:, None, :]).reshape(
        2 * tile_width * tile_width
    )
    local_energy = lax.dynamic_slice_in_dim(
        virt_energy, lax.axis_index("virt") * column_count, column_count
    )
    pair_energy = pair_energies(eps_occ, pair_list)
    return ladder / (pair_energy[:, None] - local_energy[None, :])


def any_mesh_body(amplitudes, integrals, eps_occ, eps_vir, pair_list):
    tile_width = eps_vir.shape[0] // 2
    by_pairs = lax.dot_general(
        lax.all_gather(amplitudes, "pair", axis=0, tiled=True),
        integrals,
        (((1,), (1,)), ((), ())),
        precision=lax.Precision.HIGHEST,
        preferred_element_type=jnp.float32,
    )
    partial_value = lax.all_to_all(by_pairs, "pair", split_axis=0, concat_axis=1, tiled=True)
    ladder = sum_to_owners(antisymmetrize(partial_value, tile_width))
    return (ladder, updated(ladder, eps_occ, eps_vir, pair_list))


def split(value):
    high = value.astype(jnp.bfloat16)
    return high, (value - high.astype(jnp.float32)).astype(jnp.bfloat16)


def times(left, right):
    return lax.dot_general(
        left, right, (((1,), (1,)), ((), ())), preferred_element_type=jnp.float32
    )


def ladder_kernel(
    h, amp_ref, int_ref, out_ref, stage, int_high, int_low, blocks, weights, ct_ref,
    got, summed, rows, diff, below, above, upward, downward, kept, other, placed,
    stage_sem, amp_send, amp_recv,
    core_send, core_recv, pair_send, pair_recv, up_send, up_recv, down_send, down_recv,
    last_send, last_recv,
):
    r = lax.axis_index("pair")
    v = lax.axis_index("virt")
    z = v // 2
    c = v % 2
    mate = v + 1 - 2 * c
    x = r % 2
    y = r // 2
    peers = (y * 2 + (1 - x), (1 - y) * 2 + x, (1 - y) * 2 + (1 - x))
    count, depth = amp_ref.shape
    cut = count // 16 * 8
    parts = (pl.ds(0, cut), pl.ds(cut, count - cut))
    step = stage.shape[1]
    steps = int_ref.shape[0] // step

    def stage_copy(t):
        return pltpu.make_async_copy(
            int_ref.at[pl.ds(pl.multiple_of(t * step, 8), step)],
            stage.at[t % 2],
            stage_sem.at[t % 2],
        )

    stage_copy(0).start()
    stage_copy(1).start()

    barrier = pltpu.get_barrier_semaphore()
    pl.semaphore_signal(barrier, inc=1, device_id={"virt": mate}, device_id_type=MESH)
    for peer in peers:
        pl.semaphore_signal(barrier, inc=1, device_id={"pair": peer}, device_id_type=MESH)

    @pl.when(z < 3)
    def _():
        pl.semaphore_signal(barrier, inc=1, device_id={"virt": v + 2}, device_id_type=MESH)

    @pl.when(z > 0)
    def _():
        pl.semaphore_signal(barrier, inc=1, device_id={"virt": v - 2}, device_id_type=MESH)

    inner = jnp.logical_and(z > 0, z < 3)

    @pl.when(inner)
    def _():
        pl.semaphore_wait(barrier, 6)

    @pl.when(jnp.logical_not(inner))
    def _():
        pl.semaphore_wait(barrier, 5)

    def amp_copy(d, part):
        return pltpu.make_async_remote_copy(
            src_ref=amp_ref.at[parts[part]],
            dst_ref=blocks.at[d, parts[part]],
            send_sem=amp_send.at[d, part],
            recv_sem=amp_recv.at[d, part],
            device_id={"pair": peers[d]},
            device_id_type=MESH,
        )

    def pass_on(d):
        return pltpu.make_async_remote_copy(
            src_ref=blocks.at[d, parts[d]],
            dst_ref=blocks.at[2, parts[d]],
            send_sem=amp_send.at[2, d],
            recv_sem=amp_recv.at[2, d],
            device_id={"pair": peers[1 - d]},
            device_id_type=MESH,
        )

    for late in range(2):
        for d in range(2):
            amp_copy(d, d if late == 0 else 1 - d).start()

    def weigh(source, high_at, low_at):
        wide = 2 * LANES

        @pl.loop(0, depth // wide)
        def _(k):
            columns = pl.ds(pl.multiple_of(k * wide, wide), wide)
            value = source[:, columns]
            if count < LANES:
                value = jnp.concatenate(
                    [value, jnp.zeros((LANES - count, wide), jnp.float32)], axis=0
                )
            high, low = split(value)
            weights[pl.ds(high_at * LANES, LANES), columns] = high
            weights[pl.ds(low_at * LANES, LANES), columns] = low

    def keep(t, size, lanes, value):
        per = size // (4 * h)
        i = t // (h // per)
        at = pl.multiple_of(t % (h // per) * per, per)
        ct_ref[i, pl.ds(at, per), :, :, :, lanes] = value.reshape(per, 2, 2, h, value.shape[1])

    def one_block(high, low, at):
        both = times(high, weights[pl.ds(at * LANES, 2 * LANES), :])
        rest = times(low, weights[pl.ds(at * LANES, LANES), :])
        return both[:, :LANES] + both[:, LANES:] + rest

    weigh(amp_ref, 0, 1)

    @pl.loop(0, steps)
    def _(t):
        stage_copy(t).wait()
        high, low = split(stage[t % 2])
        at = pl.ds(pl.multiple_of(t * step, 16), step)
        int_high[at, :] = high
        int_low[at, :] = low

        @pl.when(t + 2 < steps)
        def _():
            stage_copy(t + 2).start()

        keep(t, step, pl.ds(3 * LANES, LANES), one_block(int_high[at, :], int_low[at, :], 0))

    for d in range(2):
        amp_copy(d, d).wait_recv()
        pass_on(d).start()

    order = (peers[2], peers[0], peers[1], r)

    def core_copy(n, i):
        return pltpu.make_async_remote_copy(
            src_ref=ct_ref.at[i, :, :, (1 - c + i) % 2, :, pl.ds(n * LANES, LANES)],
            dst_ref=got.at[n, i],
            send_sem=core_send.at[n, i],
            recv_sem=core_recv.at[n, i],
            device_id={"virt": mate},
            device_id_type=MESH,
        )

    def pair_copy(n, piece):
        bh = jnp.where(piece == 0, 1 - x, x) if n == 1 else piece
        return pltpu.make_async_remote_copy(
            src_ref=summed.at[n, :, bh],
            dst_ref=rows.at[r, :, bh],
            send_sem=pair_send.at[n, piece],
            recv_sem=pair_recv.at[n, piece],
            device_id={"pair": order[n]},
            device_id_type=MESH,
        )

    def pair_arrived(n, piece):
        pair_copy(n, piece).wait_recv()

    def core_start(n):
        for i in range(2):
            core_copy(n, i).start()

    half = steps // 4

    def core_add(n):
        lanes = pl.ds(n * LANES, LANES)
        for i in range(2):
            core_copy(n, i).wait_recv()

            @pl.loop(0, h, unroll=4)
            def _(a):
                for bh in range(2):
                    total = ct_ref[i, a, bh, (c + i) % 2, :, lanes] + got[n, i, a, bh]
                    if n < 3:
                        summed[n, i * h + a, bh] = total
                    else:
                        rows[r, i * h + a, bh] = total

    core_start(3)
    for d in range(2):
        amp_copy(d, 1 - d).wait_recv()
        weigh(blocks.at[d], 4 + d, 6 + d)
    big = 2 * step

    for i in range(2):

        @pl.loop(i * half, (i + 1) * half)
        def _(t):
            at = pl.ds(pl.multiple_of(t * big, 16), big)
            near_high = weights[pl.ds(4 * LANES, 2 * LANES), :]
            near_low = weights[pl.ds(6 * LANES, 2 * LANES), :]
            value = times(int_high[at, :], near_high) + times(int_high[at, :], near_low)
            value = value + times(int_low[at, :], near_high)
            keep(t, big, pl.ds(LANES, 2 * LANES), value)

        core_copy(1, i).start()
        core_copy(2, i).start()

    core_add(1)
    pair_copy(1, 0).start()
    core_add(2)
    pair_copy(2, 0).start()
    pair_copy(2, 1).start()
    pair_copy(1, 1).start()
    core_add(3)
    for d in range(2):
        pass_on(d).wait_recv()
    weigh(blocks.at[2], 2, 3)

    @pl.loop(0, steps // 2)
    def _(t):
        at = pl.ds(pl.multiple_of(t * big, 16), big)
        keep(t, big, pl.ds(0, LANES), one_block(int_high[at, :], int_low[at, :], 2))

    core_start(0)
    core_add(0)
    pair_copy(0, 0).start()
    pair_copy(0, 1).start()

    def antisym(q, i, u):
        ah = q // 2
        bh = q % 2
        mirror = (c + i) % 2

        @pl.loop(0, h // 2, unroll=4)
        def _(n):
            a = u * (h // 2) + n
            plain = rows[ah, i * h + a, bh]
            turned = rows[2 + bh, pl.ds(mirror * h, h), ah, a, :]
            diff[q * 4 + i * 2 + u, pl.ds(pl.multiple_of(n * h, 8), h), :] = plain - turned

    def up_copy(q):
        return pltpu.make_async_remote_copy(
            src_ref=upward.at[q], dst_ref=below.at[q],
            send_sem=up_send.at[q], recv_sem=up_recv.at[q],
            device_id={"virt": v + 2}, device_id_type=MESH,
        )

    def down_copy(q):
        return pltpu.make_async_remote_copy(
            src_ref=downward.at[q], dst_ref=above.at[q],
            send_sem=down_send.at[q], recv_sem=down_recv.at[q],
            device_id={"virt": v - 2}, device_id_type=MESH,
        )

    def sends_up(q):
        return jnp.logical_or(z < 2, jnp.logical_and(z == 2, q // 4 % 2 == 1))

    def sends_down(q):
        return jnp.logical_or(z > 1, jnp.logical_and(z == 1, q // 8 == 0))

    def hears_below(q):
        return jnp.logical_or(inner, jnp.logical_and(z == 3, q // 4 % 2 == 1))

    def hears_above(q):
        return jnp.logical_or(inner, jnp.logical_and(z == 0, q // 8 == 0))

    def go_up(q):
        @pl.when(hears_below(q))
        def _():
            up_copy(q).wait_recv()

        @pl.when(z == 0)
        def _():
            upward[q] = diff[q]

        @pl.when(jnp.logical_and(z > 0, sends_up(q)))
        def _():
            upward[q] = diff[q] + below[q]

        @pl.when(sends_up(q))
        def _():
            up_copy(q).start()

    def go_down(q):
        @pl.when(hears_above(q))
        def _():
            down_copy(q).wait_recv()

        @pl.when(z == 3)
        def _():
            downward[q] = diff[q]

        @pl.when(jnp.logical_and(z < 3, sends_down(q)))
        def _():
            downward[q] = diff[q] + above[q]

        @pl.when(sends_down(q))
        def _():
            down_copy(q).start()

    def near(q):
        @pl.when(z < 2)
        def _():
            go_up(q)

        @pl.when(z >= 2)
        def _():
            go_down(q)

    def far(q):
        @pl.when(z < 2)
        def _():
            go_down(q)

        @pl.when(z >= 2)
        def _():
            go_up(q)

    early = [jnp.where(y == 0, t * 2 + x, x * 2 + t) for t in range(2)]
    late = [jnp.where(y == 0, t * 2 + 1 - x, (1 - x) * 2 + t) for t in range(2)]
    quads = early + late
    chunks = [q * 4 + n for q in quads for n in range(4)]
    needs = (((1, 0), (2, 0)), ((2, 1),), ((1, 1), (0, 0)), ((0, 1),))
    lag = 3
    for s in range(16):
        if s % 4 == 0:
            for n, piece in needs[s // 4]:
                pair_arrived(n, piece)
        antisym(quads[s // 4], s // 2 % 2, s % 2)
        near(chunks[s])
        if s >= lag:

            @pl.when(inner)
            def _():
                far(chunks[s - lag])

    @pl.when(jnp.logical_not(inner))
    def _():
        for s in range(16 - lag):
            far(chunks[s])

    for s in range(16 - lag, 16):
        far(chunks[s])

    def total_of(t, i):
        q = pl.ds(jnp.where(z < 2, z * 2 + t, t * 2 + z - 2) * 4 + i * 2, 2)
        low = jnp.where(z > 0, below[q], jnp.float32(0.0))
        high = jnp.where(z < 3, above[q], jnp.float32(0.0))
        return (diff[q] + low + high).reshape(h * h, LANES)

    mine = jnp.where(z < 2, c, 0)
    for t in range(2):
        other[t] = total_of(t, jnp.where(z < 2, 1 - c, 1))
    last = pltpu.make_async_remote_copy(
        src_ref=other, dst_ref=kept.at[1], send_sem=last_send, recv_sem=last_recv,
        device_id={"virt": mate}, device_id_type=MESH,
    )
    last.start()
    for t in range(2):
        kept[0, t] = total_of(t, mine)

    def put(s):
        for t in range(2):

            @pl.loop(0, h, unroll=4)
            def _(a):
                at = pl.multiple_of((a * 4 + 2 * t + s) * h, 8)
                plain = kept[s, t, pl.ds(pl.multiple_of(a * h, 8), h), :]
                turned = kept[s, t, pl.ds(a, h, stride=h), :]
                placed[pl.ds(at, h), :] = jnp.where(z < 2, plain, turned)

    put(0)
    last.wait_recv()
    put(1)

    for n in range(out_ref.shape[1] // LANES):
        at = pl.ds(n * LANES, LANES)
        out_ref[:, at] = placed[at, :].T[:count]

    last.wait_send()
    for d in range(2):
        amp_copy(d, 0).wait_send()
        amp_copy(d, 1).wait_send()
        pass_on(d).wait_send()
    for n in range(4):
        for i in range(2):
            core_copy(n, i).wait_send()
    for n in range(3):
        for piece in range(2):
            pair_copy(n, piece).wait_send()
    for q in range(16):

        @pl.when(sends_up(q))
        def _():
            up_copy(q).wait_send()

        @pl.when(sends_down(q))
        def _():
            down_copy(q).wait_send()


def ladder_of(amplitudes, integrals, tile_width):
    h = tile_width // 4
    count, depth = amplitudes.shape
    owned = integrals.shape[0]
    step = owned // 8
    f32 = jnp.float32
    bf16 = jnp.bfloat16
    dma = pltpu.SemaphoreType.DMA
    return pl.pallas_call(
        functools.partial(ladder_kernel, h),
        out_shape=jax.ShapeDtypeStruct((count, tile_width * h), f32),
        in_specs=[pl.BlockSpec(memory_space=pltpu.VMEM), pl.BlockSpec(memory_space=pl.ANY)],
        out_specs=pl.BlockSpec(memory_space=pltpu.VMEM),
        scratch_shapes=[
            pltpu.VMEM((2, step, depth), f32),
            pltpu.VMEM((owned, depth), bf16),
            pltpu.VMEM((owned, depth), bf16),
            pltpu.VMEM((3, count, depth), f32),
            pltpu.VMEM((8 * LANES, depth), bf16),
            pltpu.VMEM((2, h, 2, 2, h, 4 * LANES), f32),
            pltpu.VMEM((4, 2, h, 2, h, LANES), f32),
            pltpu.VMEM((3, 2 * h, 2, h, LANES), f32),
            pltpu.VMEM((4, 2 * h, 2, h, LANES), f32),
            pltpu.VMEM((16, h * h // 2, LANES), f32),
            pltpu.VMEM((16, h * h // 2, LANES), f32),
            pltpu.VMEM((16, h * h // 2, LANES), f32),
            pltpu.VMEM((16, h * h // 2, LANES), f32),
            pltpu.VMEM((16, h * h // 2, LANES), f32),
            pltpu.VMEM((2, 2, h * h, LANES), f32),
            pltpu.VMEM((2, h * h, LANES), f32),
            pltpu.VMEM((tile_width * h, LANES), f32),
            dma((2,)), dma((3, 2)), dma((3, 2)),
            dma((4, 2)), dma((4, 2)), dma((3, 2)), dma((3, 2)),
            dma((16,)), dma((16,)), dma((16,)), dma((16,)), dma, dma,
        ],
        compiler_params=pltpu.CompilerParams(
            collective_id=0, has_side_effects=True, vmem_limit_bytes=60 * 1024 * 1024
        ),
        name="ladder",
    )(amplitudes, integrals)


def block_body(amplitudes, integrals, eps_occ, eps_vir, pair_list):
    tile_width = eps_vir.shape[0] // 2
    first = lax.axis_index("virt") < lax.axis_size("virt") // 2
    sign = jnp.where(first, jnp.float32(1.0), jnp.float32(-1.0))
    raw = ladder_of(amplitudes, integrals, tile_width)
    raw, eps_occ, eps_vir, pair_list = lax.optimization_barrier(
        (raw, eps_occ, eps_vir, pair_list)
    )
    ladder = sign * raw
    return (ladder, updated(ladder, eps_occ, eps_vir, pair_list))


def solution(mesh):
    in_specs = (P("pair", "virt"), P("pair", "virt"), P(), P(), P("pair", None))
    out_specs = (P("pair", "virt"), P("pair", "virt"))
    fits = mesh.shape["pair"] == 4 and mesh.shape["virt"] == 8

    def body(amplitudes, integrals, eps_occ, eps_vir, pair_list):
        tiled = eps_vir.shape[0] % 64 == 0 and amplitudes.shape[0] <= LANES
        chosen = block_body if fits and tiled else any_mesh_body
        return chosen(amplitudes, integrals, eps_occ, eps_vir, pair_list)

    return jax.shard_map(body, mesh=mesh, in_specs=in_specs, out_specs=out_specs, check_vma=False)
```
